512 devices in a mesh: expert: 32 (over y, z_lo, core), tensor: 16 (over x, z_hi).
Axes of the slice: x: 4, y: 8, z: 8 (z_hi: 4, z_lo: 2; z = z_hi * 2 + z_lo), core: 2. Of those that a mesh axis runs over, the one named last changes fastest.
Arguments:
- tokens: bfloat16 [4096, 6144], P('expert', 'tensor'), may hold values from -6 to 6
- expert_ids: int32 [4096, 2], P('expert'), may hold values from 0 to 7, all different within a row; in each aligned block of 128 rows (0 to 127, 128 to 255, ...) at most 48 rows name the same one
- gate_fixed: int32 [4096, 2], P('expert'), may hold values from 4096 to 65535
- w_gate: bfloat16 [32, 1024, 6144], P('expert', None, 'tensor'), may hold values from -0.078125 to 0.078125
- w_up: bfloat16 [32, 1024, 6144], P('expert', None, 'tensor'), may hold values from -0.078125 to 0.078125
- w_down: bfloat16 [32, 1024, 6144], P('expert', None, 'tensor'), may hold values from -0.0625 to 0.0625
Outputs:
- mixed: bfloat16 [4096, 6144], P('expert', 'tensor')
The draws below stay inside these ranges and needn't reach their ends.
Inputs may be any that keep to these rules, and one draw needn't show every extreme that they name: `expert_ids`: each row names 2 different experts. Among the 128 rows of one sequence shard (aligned blocks), no expert is named by more than 48 rows, a bound that some block reaches.
All inputs are finite; a program needn't handle non-finite values.
Results may differ from the reference program's by a relative error of at most 0.0064.
Values may be sent and summed in bfloat16 or wider, within the bound.
No kernel may reach another device: no remote copies, remote signals or barrier semaphores. Data moves between devices by JAX's collectives and lax.ppermute only.
A program may use at most 64 MiB of HBM per device.

```python
import math
import jax
import jax.numpy as jnp
import numpy as np
from jax import lax

D = 6144
FFW = 8192
ROUTED = 8
EXPERTS = 4
TOP = 2
TOK_SH = 128
CAP = 48
QUART = 8
FQ = 1024
DT = 384
TOKENS = 4096
N_EXPERT = 32


def set_ends(entries, stream_key, least, largest):
    place = [jax.random.randint(jax.random.fold_in(stream_key, axis), (), 0, length) for axis, length in enumerate(entries.shape)]
    longest = entries.shape.index(max(entries.shape))
    beside = place[:longest] + [(place[longest] + 1) % entries.shape[longest]] + place[longest + 1:]
    return entries.at[tuple(place)].set(least).at[tuple(beside)].set(largest)


def steps_of(own_key, extent, cuts, low, high):
    factor_of, own = 1.0, jax.random.fold_in(own_key, 6)
    for dim, blocks in cuts:
        draws = jnp.exp(jax.random.uniform(jax.random.fold_in(own, dim), (blocks,), jnp.float32, low / len(cuts), high / len(cuts)))
        factor_of = factor_of * jnp.repeat(draws, extent[dim] // blocks).reshape([-1 if axis == dim else 1 for axis in range(len(extent))])
    return factor_of


def assign_block(stream_key, own, number, rows, number_of, top, limit, slope):
    order = jax.random.permutation(stream_key, number_of)
    packed, ordinary = shares(number_of, rows * top, limit, slope, True), shares(number_of, rows * top, limit, slope, False)
    places = jnp.arange(number_of)

    def named(tallies, rotation):
        used = int((tallies > 0).sum())
        fixed = max(1, used // 4)
        moved = fixed + (places - fixed + rotation * (used - fixed)) % max(1, number_of - fixed)
        return jnp.zeros((number_of,), jnp.int32).at[order[jnp.where(places < fixed, places, moved)]].set(jnp.asarray(tallies, jnp.int32))

    tallies = jnp.where(number % 4 == 0, named(packed, number // 4), named(ordinary, number - number // 4 - 1))
    mixed = jax.random.permutation(jax.random.fold_in(own, 3), number_of)
    source_of, receiver = mixed[0:number_of // 2 * 2:2], mixed[1:number_of // 2 * 2:2]
    slack = jnp.minimum(tallies[source_of] - 1, limit - tallies[receiver]) // 2
    slack = jnp.where((source_of == order[0]) | (receiver == order[0]) | (tallies[receiver] == 0), 0, jnp.maximum(slack, 0))
    moved = jax.random.randint(jax.random.fold_in(own, 4), (number_of // 2,), 0, 1 << 20) % (slack + 1)
    tallies = tallies.at[source_of].add(-moved).at[receiver].add(moved)
    labels = jnp.searchsorted(jnp.cumsum(tallies), jnp.arange(rows * top), side="right").astype(jnp.int32)
    listing = labels.reshape(top, rows).T
    listing = listing[jax.random.permutation(jax.random.fold_in(own, 1), rows)]
    rotation = jax.random.randint(jax.random.fold_in(own, 2), (rows, 1), 0, top)
    return jnp.take_along_axis(listing, (jnp.arange(top)[None, :] + rotation) % top, axis=1)


def shares(amount, total, most, slope, full):
    weights = [(1 << 20) // math.isqrt(standing ** slope) + 1 for standing in range(1, amount + 1)]
    largest = most if full else min(most, max(-(-total // amount), total * weights[0] // sum(weights)))
    least = 1 if total - largest >= amount - 1 else 0
    given, spare = [largest] + [least] * (amount - 1), total - largest - least * (amount - 1)
    while spare > 0:
        movable = [i for i in range(1, amount) if given[i] < largest] or [i for i in range(1, amount) if given[i] < most]
        mass, left = sum([weights[i] for i in movable]), spare
        for i in movable:
            more = min(most - given[i], max(1, left * weights[i] // mass), spare)
            given[i] = given[i] + more
            spare = spare - more
    return np.array(given)


def bell_draw(key, shape, spread, bound, shards=(), kind=jnp.bfloat16):
    entries = jax.random.normal(key, shape, jnp.float32) * spread
    if len(shards) > 0:
        entries = steps_of(key, shape, shards, -0.22, 0.18) * entries
    return jnp.clip(entries, min=-bound, max=bound).astype(kind)


def setup_inputs(seed: int = 0) -> dict:
    keys = jax.random.split(jax.random.key(seed), 7)
    tokens = bell_draw(keys[0], (TOKENS, D), 1.0, 6.0, ((0, 32), (1, 16)))
    expert_ids_keys = jax.random.split(jax.random.fold_in(keys[1], 1), TOKENS // TOK_SH)
    expert_ids_turns = jax.random.permutation(jax.random.fold_in(keys[1], 3), TOKENS // TOK_SH)
    expert_ids = jax.vmap(lambda own, number: assign_block(jax.random.fold_in(keys[1], 2), own, number, TOK_SH, ROUTED, TOP, CAP, 2))(expert_ids_keys, expert_ids_turns).reshape((TOKENS, TOP))
    gate_fixed = set_ends(jax.random.randint(keys[2], (TOKENS, TOP), 4096, 65536), jax.random.fold_in(keys[2], 1), 4096, 65535).astype(jnp.int32)
    w_gate = bell_draw(keys[3], (QUART * EXPERTS, FQ, D), D ** -0.5, 0.078125, ((0, 32), (2, 16)))
    w_up = bell_draw(keys[4], (QUART * EXPERTS, FQ, D), D ** -0.5, 0.078125, ((0, 32), (2, 16)))
    w_down = bell_draw(keys[5], (QUART * EXPERTS, FQ, D), FFW ** -0.5, 0.0625, ((0, 32), (2, 16)))
    return dict(tokens=tokens, expert_ids=expert_ids, gate_fixed=gate_fixed, w_gate=w_gate, w_up=w_up, w_down=w_down)


def expert_rows(token_blocks, gate_matrix, up_matrix, down_matrix):
    gate_blocks = gate_matrix.reshape(FFW, D // DT, DT)
    up_blocks = up_matrix.reshape(FFW, D // DT, DT)
    contract = (((1,), (1,)), ((), ()))

    def add_block(running, block_index):
        gate_sum, up_sum = running
        token_part = lax.dynamic_index_in_dim(token_blocks, block_index, 1, keepdims=False)
        gate_part = lax.dynamic_index_in_dim(gate_blocks, block_index, 1, keepdims=False)
        up_part = lax.dynamic_index_in_dim(up_blocks, block_index, 1, keepdims=False)
        gate_term = lax.dot_general(token_part, gate_part, contract, preferred_element_type=jnp.float32)
        up_term = lax.dot_general(token_part, up_part, contract, preferred_element_type=jnp.float32)
        gate_term = lax.optimization_barrier(gate_term.astype(jnp.bfloat16)).astype(jnp.float32)
        up_term = lax.optimization_barrier(up_term.astype(jnp.bfloat16)).astype(jnp.float32)
        return (gate_sum + gate_term, up_sum + up_term), None

    empty_sum = jnp.zeros((token_blocks.shape[0], FFW), jnp.float32)
    block_list = jnp.arange(D // DT, dtype=jnp.int32)
    (gate_sum, up_sum), _ = lax.scan(add_block, (empty_sum, empty_sum), block_list)
    hidden = (jax.nn.silu(gate_sum) * up_sum).astype(jnp.bfloat16)
    return jnp.dot(hidden, down_matrix, preferred_element_type=jnp.float32)


def reference(tokens, expert_ids, gate_fixed, w_gate, w_up, w_down):
    quarters = N_EXPERT // EXPERTS
    slots = N_EXPERT * CAP

    def regroup(weight_arr):
        return weight_arr.reshape(quarters, EXPERTS, FQ, D).transpose(1, 0, 2, 3).reshape(EXPERTS, FFW, D)

    token_blocks = tokens.reshape(TOKENS, D // DT, DT)
    slot_iota = jnp.arange(slots, dtype=jnp.int32)

    def one_expert(total, weight_set):
        gate_matrix, up_matrix, down_matrix, which = weight_set
        matched = expert_ids == which
        weight = jnp.sum(jnp.where(matched, gate_fixed, 0), axis=1).astype(jnp.float32) / 65536.0
        hit = jnp.any(matched, axis=1)
        count = jnp.sum(hit.astype(jnp.int32))
        index = jnp.nonzero(hit, size=slots, fill_value=0)[0].astype(jnp.int32)
        row_weight = jnp.where(slot_iota < count, weight[index], jnp.float32(0.0))
        out = expert_rows(token_blocks[index], gate_matrix, up_matrix, down_matrix)
        return total.at[index].add(out * row_weight[:, None]), None

    which_list = jnp.arange(EXPERTS, dtype=jnp.int32)
    start = jnp.zeros((TOKENS, D), jnp.float32)
    mixed, _ = lax.scan(one_expert, start, (regroup(w_gate), regroup(w_up), regroup(w_down), which_list))
    return mixed.astype(jnp.bfloat16)
```

```python
import jax
import jax.numpy as jnp
from jax import lax
from jax.sharding import Mesh
from jax.sharding import PartitionSpec as P

EXPERTS = 4
CAP = 48
LOCAL = ("zl", "core")


def shift(array, axis, step):
    size = lax.axis_size(axis)
    return lax.ppermute(array, axis, [(i, (i + step) % size) for i in range(size)])


def spread(weight):
    return (weight, shift(weight, "x", -1), shift(weight, "x", 2), shift(weight, "x", 1))


def on_device(tokens, expert_ids, gate_fixed, w_gate, w_up, w_down):
    width_part = tokens.shape[1]
    x_size = lax.axis_size("x")
    y_size = lax.axis_size("y")
    zh_size = lax.axis_size("zh")
    x_own = lax.axis_index("x")
    shard_own = lax.axis_index(LOCAL)
    expert_iota = jnp.arange(EXPERTS, dtype=jnp.int32)
    matched = expert_ids[:, :, None] == expert_iota
    routed = jnp.sum(matched.astype(jnp.int32), axis=1)
    weights = (
        jnp.sum(jnp.where(matched, gate_fixed[:, :, None], 0), axis=1).astype(jnp.float32) / 65536.0
    )
    position = jnp.cumsum(routed, axis=0) - routed
    slot_iota = jnp.arange(CAP, dtype=jnp.int32)
    placed = (position[:, :, None] == slot_iota) & (routed[:, :, None] > 0)
    outgoing = jnp.einsum(
        "tec,td->ecd", placed.astype(jnp.bfloat16), tokens, preferred_element_type=jnp.float32
    ).astype(jnp.bfloat16)
    outgoing, gate_own = lax.optimization_barrier((outgoing, w_gate[0]))
    gate_all = spread(gate_own)
    sent = jnp.broadcast_to(outgoing[:, None], (EXPERTS, x_size, CAP, width_part))
    local = lax.all_to_all(
        sent.reshape(EXPERTS * x_size, CAP, width_part),
        LOCAL + ("x",),
        split_axis=0,
        concat_axis=0,
        tiled=True,
    ).reshape(EXPERTS, x_size, CAP, width_part)
    mine = lax.dynamic_index_in_dim(local, x_own, 0, keepdims=False)
    order = [(x_own + step) % x_size for step in range(x_size)]
    mine = jnp.stack([lax.dynamic_index_in_dim(mine, place, 0, keepdims=False) for place in order])
    sent_y = jnp.broadcast_to(mine[None], (y_size, x_size, CAP, width_part))
    rows = lax.all_to_all(sent_y, "y", split_axis=0, concat_axis=0, tiled=True)
    total_rows = y_size * CAP
    rows = [rows[:, step].reshape(total_rows, width_part) for step in range(x_size)]
    contract = (((1,), (1,)), ((), ()))

    def project(blocks):
        total = None
        for row_block, block in zip(rows, blocks):
            term = lax.dot_general(row_block, block, contract, preferred_element_type=jnp.float32)
            total = term if total is None else total + term
        return total.astype(jnp.bfloat16)

    def share(term):
        parts = lax.all_to_all(term, "zh", split_axis=0, concat_axis=0, tiled=True)
        parts = parts.reshape(zh_size, total_rows // zh_size, -1)
        return jnp.sum(parts.astype(jnp.float32), axis=0)

    gate_term = project(gate_all)
    up_own, _ = lax.optimization_barrier((w_up[0], gate_all[2]))
    up_all = spread(up_own)
    gate_share = share(gate_term)
    up_term = project(up_all)
    down_own, _ = lax.optimization_barrier((w_down[0], up_all[2]))
    down_all = spread(down_own)
    up_share = share(up_term)
    hidden = (jax.nn.silu(gate_share) * up_share).astype(jnp.bfloat16)
    hidden_rows = lax.all_to_all(
        jnp.broadcast_to(hidden[None], (zh_size,) + hidden.shape),
        "zh",
        split_axis=0,
        concat_axis=0,
        tiled=True,
    ).reshape(total_rows, -1)
    outs = [
        jnp.dot(hidden_rows, block, preferred_element_type=jnp.float32)
        .astype(jnp.bfloat16)
        .reshape(y_size, CAP, width_part)
        for block in down_all
    ]
    back = lax.all_to_all(jnp.stack(outs, axis=1), "y", split_axis=0, concat_axis=0, tiled=True)
    back = jnp.sum(back.astype(jnp.float32), axis=0).astype(jnp.bfloat16)
    back = jnp.stack(
        [
            lax.dynamic_index_in_dim(back, (place - x_own) % x_size, 0, keepdims=False)
            for place in range(x_size)
        ]
    )
    back = jnp.broadcast_to(back[None], (EXPERTS, x_size, CAP, width_part))
    final = lax.all_to_all(
        back.reshape(EXPERTS * x_size, CAP, width_part),
        LOCAL + ("x",),
        split_axis=0,
        concat_axis=0,
        tiled=True,
    ).reshape(EXPERTS, x_size, CAP, width_part)
    summed = lax.dynamic_index_in_dim(final, shard_own, 1, keepdims=False).astype(jnp.float32)
    selector = placed.astype(jnp.float32) * weights[:, :, None]
    mixed = jnp.einsum("tec,ecd->td", selector, summed, precision=lax.Precision.HIGHEST)
    return mixed.astype(jnp.bfloat16)


def solution(mesh):
    expert, tensor = mesh.devices.shape
    fine = Mesh(
        mesh.devices.reshape(expert // 4, 2, 2, 4, tensor // 4), ("y", "zl", "core", "x", "zh")
    )
    rows, cols = ("y", "zl", "core"), ("x", "zh")
    placed = (
        P(rows, cols),
        P(rows, None),
        P(rows, None),
        P(rows, None, cols),
        P(rows, None, cols),
        P(rows, None, cols),
    )
    return jax.shard_map(
        on_device, mesh=fine, in_specs=placed, out_specs=P(rows, cols), check_vma=False
    )
```

```python
import jax
import jax.numpy as jnp
from jax import lax
from jax.sharding import Mesh
from jax.sharding import PartitionSpec as P


EXPERTS = 4
CAP = 48
LOCAL = ("zl", "core")


def shift(array, axis, step):
    size = lax.axis_size(axis)
    return lax.ppermute(array, axis, [(i, (i + step) % size) for i in range(size)])


def spread(weight):
    after = shift(weight, "x", -1)
    before = shift(weight, "x", 1)
    across = shift(weight, "x", 2)
    return (weight, after, across, before)


def on_device(tokens, expert_ids, gate_fixed, w_gate, w_up, w_down):
    width_part = tokens.shape[1]
    x_size = lax.axis_size("x")
    y_size = lax.axis_size("y")
    zh_size = lax.axis_size("zh")
    x_own = lax.axis_index("x")
    expert_iota = jnp.arange(EXPERTS, dtype=jnp.int32)
    matched = expert_ids[:, :, None] == expert_iota
    routed = jnp.sum(matched.astype(jnp.int32), axis=1)
    weights = (
        jnp.sum(jnp.where(matched, gate_fixed[:, :, None], 0), axis=1).astype(jnp.float32) / 65536.0
    )
    position = jnp.cumsum(routed, axis=0) - routed
    slot_iota = jnp.arange(CAP, dtype=jnp.int32)
    placed = (position[:, :, None] == slot_iota) & (routed[:, :, None] > 0)
    outgoing = jnp.einsum(
        "tec,td->ecd", placed.astype(jnp.bfloat16), tokens, preferred_element_type=jnp.float32
    ).astype(jnp.bfloat16)
    gate_all = spread(w_gate[0])
    sent = jnp.broadcast_to(outgoing[:, None], (EXPERTS, x_size, CAP, width_part))
    local = lax.all_to_all(
        sent.reshape(EXPERTS * x_size, CAP, width_part),
        LOCAL + ("x",),
        split_axis=0,
        concat_axis=0,
        tiled=True,
    ).reshape(EXPERTS, x_size, CAP, width_part)
    order = [(x_own + step) % x_size for step in range(x_size)]
    mine = lax.dynamic_index_in_dim(local, x_own, 0, keepdims=False)
    mine = jnp.stack([lax.dynamic_index_in_dim(mine, place, 0, keepdims=False) for place in order])
    sent_y = jnp.broadcast_to(mine[None], (y_size, x_size, CAP, width_part))
    rows = lax.all_to_all(sent_y, "y", split_axis=0, concat_axis=0, tiled=True)
    total_rows = y_size * CAP
    rows = [rows[:, step].reshape(total_rows, width_part) for step in range(x_size)]
    contract = (((1,), (1,)), ((), ()))

    def project(blocks):
        total = None
        for row_block, block in zip(rows, blocks):
            term = lax.dot_general(row_block, block, contract, preferred_element_type=jnp.float32)
            term = lax.reduce_precision(term, 8, 7)
            total = term if total is None else total + term
        return total.astype(jnp.bfloat16)

    def share(term):
        parts = lax.all_to_all(term, "zh", split_axis=0, concat_axis=0, tiled=True)
        parts = parts.reshape(zh_size, total_rows // zh_size, -1)
        return jnp.sum(parts.astype(jnp.float32), axis=0)

    gate_term = project(gate_all)
    up_own, gate_all = lax.optimization_barrier((w_up[0], gate_all))
    up_all = spread(up_own)
    gate_share = share(gate_term)
    up_term = project(up_all)
    down_own, up_all = lax.optimization_barrier((w_down[0], up_all))
    down_all = spread(down_own)
    up_share = share(up_term)
    hidden = (jax.nn.silu(gate_share) * up_share).astype(jnp.bfloat16)
    hidden_rows = lax.all_to_all(
        jnp.broadcast_to(hidden[None], (zh_size,) + hidden.shape),
        "zh",
        split_axis=0,
        concat_axis=0,
        tiled=True,
    ).reshape(total_rows, -1)
    back = jnp.zeros((y_size, x_size, CAP, width_part), jnp.bfloat16)
    for step, block in enumerate(down_all):
        out = jnp.dot(hidden_rows, block, preferred_element_type=jnp.float32).astype(jnp.bfloat16)
        out = out.reshape(y_size, 1, CAP, width_part)
        back = lax.dynamic_update_slice(back, out, (0, order[step], 0, 0))
    back = lax.all_to_all(
        back.reshape(y_size * x_size, CAP, width_part),
        ("y", "x"),
        split_axis=0,
        concat_axis=0,
        tiled=True,
    ).reshape(y_size, x_size, CAP, width_part)
    back = jnp.sum(back.astype(jnp.float32), axis=0).astype(jnp.bfloat16)
    summed = lax.all_to_all(back, LOCAL, split_axis=0, concat_axis=0, tiled=True)
    summed = summed.astype(jnp.float32)
    selector = placed.astype(jnp.float32) * weights[:, :, None]
    mixed = jnp.einsum("tec,ecd->td", selector, summed, precision=lax.Precision.HIGHEST)
    return mixed.astype(jnp.bfloat16)


def solution(mesh):
    expert, tensor = mesh.devices.shape
    fine = Mesh(
        mesh.devices.reshape(expert // 4, 2, 2, 4, tensor // 4), ("y", "zl", "core", "x", "zh")
    )
    rows, cols = ("y", "zl", "core"), ("x", "zh")
    placed = (
        P(rows, cols),
        P(rows, None),
        P(rows, None),
        P(rows, None, cols),
        P(rows, None, cols),
        P(rows, None, cols),
    )

    return jax.shard_map(
        on_device, mesh=fine, in_specs=placed, out_specs=P(rows, cols), check_vma=False
    )
```

```python
import jax
import jax.numpy as jnp
from jax import lax
from jax.experimental import pallas as pl
from jax.experimental.pallas import tpu as pltpu
from jax.sharding import Mesh
from jax.sharding import PartitionSpec as P


EXPERTS = 4
CAP = 48
LOCAL = ("zl", "core")
TILE = 256
GRANT = 16 << 20


def shift(array, axis, step):
    size = lax.axis_size(axis)
    return lax.ppermute(array, axis, [(i, (i + step) % size) for i in range(size)])


def beside(weight):
    return shift(weight, "x", -1), shift(weight, "x", 1)


def across(pair):
    after, before = pair
    half = after.shape[0] // 2
    return shift(after[:half], "x", -1), shift(before[half:], "x", 1)


def project_kernel(rows_ref, own_ref, after_ref, low_ref, high_ref, before_ref, out_ref):
    in_low = pl.program_id(0) < pl.num_programs(0) // 2
    opposite = jnp.where(in_low, low_ref[...], high_ref[...])
    blocks = (own_ref[...], after_ref[...], opposite, before_ref[...])
    sources, _, cap, depth = rows_ref.shape
    total = None
    for step, block in enumerate(blocks):
        rows = rows_ref[:, step].reshape(sources * cap, depth)
        term = lax.dot_general(
            rows, block, (((1,), (1,)), ((), ())), preferred_element_type=jnp.float32
        )
        term = term.astype(jnp.bfloat16).astype(jnp.float32)
        total = term if total is None else total + term
    out_ref[...] = total.astype(jnp.bfloat16)


def project(rows, own, pair, halves):
    sources, blocks, cap, depth = rows.shape
    width = own.shape[0]
    steps = width // TILE
    half = steps // 2
    block = (TILE, depth)
    return pl.pallas_call(
        project_kernel,
        out_shape=jax.ShapeDtypeStruct((sources * cap, width), jnp.bfloat16),
        grid=(steps,),
        in_specs=[
            pl.BlockSpec(rows.shape, lambda i: (0, 0, 0, 0)),
            pl.BlockSpec(block, lambda i: (i, 0)),
            pl.BlockSpec(block, lambda i: (i, 0)),
            pl.BlockSpec(block, lambda i: (jnp.minimum(i, half - 1), 0)),
            pl.BlockSpec(block, lambda i: (jnp.maximum(i - half, 0), 0)),
            pl.BlockSpec(block, lambda i: (i, 0)),
        ],
        out_specs=pl.BlockSpec((sources * cap, TILE), lambda i: (0, i)),
        compiler_params=pltpu.CompilerParams(vmem_limit_bytes=GRANT),
        cost_estimate=pl.CostEstimate(
            flops=2 * sources * cap * blocks * depth * width,
            bytes_accessed=2 * (rows.size + blocks * own.size + sources * cap * width),
            transcendentals=0,
        ),
    )(rows, own, pair[0], *halves, pair[1])


def expand_kernel(order_ref, hidden_ref, own_ref, after_ref, low_ref, high_ref, before_ref, out_ref):
    sources, _, cap, width = out_ref.shape
    half = low_ref.shape[0]
    hidden = hidden_ref[...]

    def put(step, value):
        value = value.astype(jnp.bfloat16).reshape(sources, cap, width)
        out_ref[:, order_ref[step]] = value

    def dot(left, right):
        return jnp.dot(left, right, preferred_element_type=jnp.float32)

    put(0, dot(hidden, own_ref[...]))
    put(1, dot(hidden, after_ref[...]))
    put(3, dot(hidden, before_ref[...]))
    put(2, dot(hidden[:, :half], low_ref[...]) + dot(hidden[:, half:], high_ref[...]))


def expand(order, hidden, own, pair, halves, sources):
    rows, width = hidden.shape
    depth = own.shape[1]
    cap = rows // sources
    places = order.shape[0]
    vmem = pl.BlockSpec(memory_space=pltpu.VMEM)
    return pl.pallas_call(
        expand_kernel,
        out_shape=jax.ShapeDtypeStruct((sources, places, cap, depth), jnp.bfloat16),
        in_specs=[pl.BlockSpec(memory_space=pltpu.SMEM)] + [vmem] * 6,
        out_specs=vmem,
        compiler_params=pltpu.CompilerParams(vmem_limit_bytes=GRANT),
        cost_estimate=pl.CostEstimate(
            flops=2 * rows * width * depth * places,
            bytes_accessed=2 * (hidden.size + places * own.size + places * rows * depth),
            transcendentals=0,
        ),
    )(order, hidden, own, pair[0], *halves, pair[1])


def on_device(tokens, expert_ids, gate_fixed, w_gate, w_up, w_down):
    width_part = tokens.shape[1]
    x_size = lax.axis_size("x")
    y_size = lax.axis_size("y")
    zh_size = lax.axis_size("zh")
    x_own = lax.axis_index("x")
    expert_iota = jnp.arange(EXPERTS, dtype=jnp.int32)
    matched = expert_ids[:, :, None] == expert_iota
    routed = jnp.sum(matched.astype(jnp.int32), axis=1)
    weights = (
        jnp.sum(jnp.where(matched, gate_fixed[:, :, None], 0), axis=1).astype(jnp.float32) / 65536.0
    )
    position = jnp.cumsum(routed, axis=0) - routed
    slot_iota = jnp.arange(CAP, dtype=jnp.int32)
    placed = (position[:, :, None] == slot_iota) & (routed[:, :, None] > 0)
    outgoing = jnp.einsum(
        "tec,td->ecd", placed.astype(jnp.bfloat16), tokens, preferred_element_type=jnp.float32
    ).astype(jnp.bfloat16)
    sent = jnp.broadcast_to(outgoing[:, None], (EXPERTS, x_size, CAP, width_part))
    local = lax.all_to_all(
        sent.reshape(EXPERTS * x_size, CAP, width_part),
        LOCAL + ("x",),
        split_axis=0,
        concat_axis=0,
        tiled=True,
    ).reshape(EXPERTS, x_size, CAP, width_part)
    order = [(x_own + step) % x_size for step in range(x_size)]
    mine = lax.dynamic_index_in_dim(local, x_own, 0, keepdims=False)
    mine = jnp.stack([lax.dynamic_index_in_dim(mine, place, 0, keepdims=False) for place in order])
    sent_y = jnp.broadcast_to(mine[None], (y_size, x_size, CAP, width_part))
    rows = lax.all_to_all(sent_y, "y", split_axis=0, concat_axis=0, tiled=True)
    total_rows = y_size * CAP

    gate_own = w_gate[0]
    gate_pair = beside(gate_own)
    gate_halves = across(gate_pair)
    up_own, _ = lax.optimization_barrier((w_up[0], gate_pair))
    up_pair = beside(up_own)
    up_halves = across(up_pair)
    down_own, _ = lax.optimization_barrier((w_down[0], up_pair))
    down_pair = beside(down_own)
    down_halves = across(down_pair)

    def share(term):
        parts = lax.all_to_all(term, "zh", split_axis=0, concat_axis=0, tiled=True)
        parts = parts.reshape(zh_size, total_rows // zh_size, -1)
        return jnp.sum(parts.astype(jnp.float32), axis=0)

    gate_term = project(rows, gate_own, gate_pair, gate_halves)
    gate_share = share(gate_term)
    up_term = project(rows, up_own, up_pair, up_halves)
    up_share = share(up_term)
    hidden = (jax.nn.silu(gate_share) * up_share).astype(jnp.bfloat16)
    hidden_rows = lax.all_gather(hidden, "zh", axis=0, tiled=True)
    back = expand(jnp.stack(order), hidden_rows, down_own, down_pair, down_halves, y_size)
    back = lax.all_to_all(
        back.reshape(y_size * x_size, CAP, width_part),
        ("y", "x"),
        split_axis=0,
        concat_axis=0,
        tiled=True,
    ).reshape(y_size, x_size, CAP, width_part)
    back = jnp.sum(back.astype(jnp.float32), axis=0).astype(jnp.bfloat16)
    summed = lax.all_to_all(back, LOCAL, split_axis=0, concat_axis=0, tiled=True)
    summed = summed.astype(jnp.float32)
    selector = placed.astype(jnp.float32) * weights[:, :, None]
    mixed = jnp.einsum("tec,ecd->td", selector, summed, precision=lax.Precision.HIGHEST)
    return mixed.astype(jnp.bfloat16)


def solution(mesh):
    expert, tensor = mesh.devices.shape
    fine = Mesh(
        mesh.devices.reshape(expert // 4, 2, 2, 4, tensor // 4), ("y", "zl", "core", "x", "zh")
    )
    rows, cols = ("y", "zl", "core"), ("x", "zh")
    placed = (
        P(rows, cols),
        P(rows, None),
        P(rows, None),
        P(rows, None, cols),
        P(rows, None, cols),
        P(rows, None, cols),
    )

    return jax.shard_map(
        on_device, mesh=fine, in_specs=placed, out_specs=P(rows, cols), check_vma=False
    )
```

```python
import jax
import jax.numpy as jnp
from jax import lax
from jax.experimental import pallas as pl
from jax.experimental.pallas import tpu as pltpu
from jax.sharding import Mesh
from jax.sharding import PartitionSpec as P


EXPERTS = 4
CAP = 48
LOCAL = ("zl", "core")
TILE = 256
GRANT = 16 << 20


def shift(array, axis, step):
    size = lax.axis_size(axis)
    return lax.ppermute(array, axis, [(i, (i + step) % size) for i in range(size)])


def beside(weight):
    return shift(weight, "x", -1), shift(weight, "x", 1)


def across(pair):
    after, before = pair
    half = after.shape[0] // 2
    return shift(after[:half], "x", -1), shift(before[half:], "x", 1)


def project_kernel(rows_ref, own_ref, after_ref, before_ref, *rest):
    *opposite_refs, out_ref = rest
    sources, blocks, cap, depth = rows_ref.shape
    part = out_ref.shape[1] // len(opposite_refs)
    rows = [rows_ref[:, step].reshape(sources * cap, depth) for step in range(blocks)]
    for start in range(0, out_ref.shape[1], TILE):
        tile = pl.ds(start, TILE)
        opposite = opposite_refs[start // part][pl.ds(start % part, TILE), :]
        total = None
        for step, block in enumerate((own_ref[tile, :], after_ref[tile, :], opposite, before_ref[tile, :])):
            term = lax.dot_general(
                rows[step], block, (((1,), (1,)), ((), ())), preferred_element_type=jnp.float32
            )
            term = term.astype(jnp.bfloat16).astype(jnp.float32)
            total = term if total is None else total + term
        out_ref[:, tile] = total.astype(jnp.bfloat16)


def project(rows, own, pair, opposite):
    sources, blocks, cap, depth = rows.shape
    width = own.shape[0]
    vmem = pl.BlockSpec(memory_space=pltpu.VMEM)
    return pl.pallas_call(
        project_kernel,
        out_shape=jax.ShapeDtypeStruct((sources * cap, width), jnp.bfloat16),
        in_specs=[vmem] * (4 + len(opposite)),
        out_specs=vmem,
        compiler_params=pltpu.CompilerParams(vmem_limit_bytes=GRANT),
        cost_estimate=pl.CostEstimate(
            flops=2 * sources * cap * blocks * depth * width,
            bytes_accessed=2 * (rows.size + blocks * own.size + sources * cap * width),
            transcendentals=0,
        ),
    )(rows, own, *pair, *opposite)


def expand_kernel(order_ref, hidden_ref, own_ref, after_ref, low_ref, high_ref, before_ref, out_ref):
    sources, _, cap, width = out_ref.shape
    half = low_ref.shape[0]
    hidden = hidden_ref[...]

    def put(step, value):
        value = value.astype(jnp.bfloat16).reshape(sources, cap, width)
        out_ref[:, order_ref[step]] = value

    def dot(left, right):
        return jnp.dot(left, right, preferred_element_type=jnp.float32)

    put(0, dot(hidden, own_ref[...]))
    put(1, dot(hidden, after_ref[...]))
    put(3, dot(hidden, before_ref[...]))
    put(2, dot(hidden[:, :half], low_ref[...]) + dot(hidden[:, half:], high_ref[...]))


def expand(order, hidden, own, pair, halves, sources):
    rows, width = hidden.shape
    depth = own.shape[1]
    cap = rows // sources
    places = order.shape[0]
    vmem = pl.BlockSpec(memory_space=pltpu.VMEM)
    return pl.pallas_call(
        expand_kernel,
        out_shape=jax.ShapeDtypeStruct((sources, places, cap, depth), jnp.bfloat16),
        in_specs=[pl.BlockSpec(memory_space=pltpu.SMEM)] + [vmem] * 6,
        out_specs=vmem,
        compiler_params=pltpu.CompilerParams(vmem_limit_bytes=GRANT),
        cost_estimate=pl.CostEstimate(
            flops=2 * rows * width * depth * places,
            bytes_accessed=2 * (hidden.size + places * own.size + places * rows * depth),
            transcendentals=0,
        ),
    )(order, hidden, own, pair[0], *halves, pair[1])


def on_device(tokens, expert_ids, gate_fixed, w_gate, w_up, w_down):
    width_part = tokens.shape[1]
    x_size = lax.axis_size("x")
    y_size = lax.axis_size("y")
    zh_size = lax.axis_size("zh")
    x_own = lax.axis_index("x")
    expert_iota = jnp.arange(EXPERTS, dtype=jnp.int32)
    matched = expert_ids[:, :, None] == expert_iota
    routed = jnp.sum(matched.astype(jnp.int32), axis=1)
    weights = (
        jnp.sum(jnp.where(matched, gate_fixed[:, :, None], 0), axis=1).astype(jnp.float32) / 65536.0
    )
    position = jnp.cumsum(routed, axis=0) - routed
    slot_iota = jnp.arange(CAP, dtype=jnp.int32)
    placed = (position[:, :, None] == slot_iota) & (routed[:, :, None] > 0)
    outgoing = jnp.einsum(
        "tec,td->ecd", placed.astype(jnp.bfloat16), tokens, preferred_element_type=jnp.float32
    ).astype(jnp.bfloat16)
    sent = jnp.broadcast_to(outgoing[:, None], (EXPERTS, x_size, CAP, width_part))
    local = lax.all_to_all(
        sent.reshape(EXPERTS * x_size, CAP, width_part),
        LOCAL + ("x",),
        split_axis=0,
        concat_axis=0,
        tiled=True,
    ).reshape(EXPERTS, x_size, CAP, width_part)
    order = [(x_own + step) % x_size for step in range(x_size)]
    mine = lax.dynamic_index_in_dim(local, x_own, 0, keepdims=False)
    mine = jnp.stack([lax.dynamic_index_in_dim(mine, place, 0, keepdims=False) for place in order])
    sent_y = jnp.broadcast_to(mine[None], (y_size, x_size, CAP, width_part))
    rows = lax.all_to_all(sent_y, "y", split_axis=0, concat_axis=0, tiled=True)
    total_rows = y_size * CAP

    gate_own = w_gate[0]
    gate_pair = beside(gate_own)
    gate_halves = across(gate_pair)
    up_own, _ = lax.optimization_barrier((w_up[0], gate_pair))
    up_pair = beside(up_own)
    up_across = (shift(up_own, "x", 2),)

    def share(term):
        parts = lax.all_to_all(term, "zh", split_axis=0, concat_axis=0, tiled=True)
        parts = parts.reshape(zh_size, total_rows // zh_size, -1)
        return jnp.sum(parts.astype(jnp.float32), axis=0)

    gate_term = project(rows, gate_own, gate_pair, gate_halves)
    gate_share = share(gate_term)
    up_term = project(rows, up_own, up_pair, up_across)
    down_own, up_term = lax.optimization_barrier((w_down[0], up_term))
    down_pair = beside(down_own)
    down_halves = across(down_pair)
    up_share = share(up_term)
    hidden = (jax.nn.silu(gate_share) * up_share).astype(jnp.bfloat16)
    hidden_rows = lax.all_gather(hidden, "zh", axis=0, tiled=True)
    back = expand(jnp.stack(order), hidden_rows, down_own, down_pair, down_halves, y_size)
    back = lax.all_to_all(
        back.reshape(y_size * x_size, CAP, width_part),
        ("y", "x"),
        split_axis=0,
        concat_axis=0,
        tiled=True,
    ).reshape(y_size, x_size, CAP, width_part)
    back = jnp.sum(back.astype(jnp.float32), axis=0).astype(jnp.bfloat16)
    summed = lax.all_to_all(back, LOCAL, split_axis=0, concat_axis=0, tiled=True)
    summed = summed.astype(jnp.float32)
    selector = placed.astype(jnp.float32) * weights[:, :, None]
    mixed = jnp.einsum("tec,ecd->td", selector, summed, precision=lax.Precision.HIGHEST)
    return mixed.astype(jnp.bfloat16)


def solution(mesh):
    expert, tensor = mesh.devices.shape
    fine = Mesh(
        mesh.devices.reshape(expert // 4, 2, 2, 4, tensor // 4), ("y", "zl", "core", "x", "zh")
    )
    rows, cols = ("y", "zl", "core"), ("x", "zh")
    placed = (
        P(rows, cols),
        P(rows, None),
        P(rows, None),
        P(rows, None, cols),
        P(rows, None, cols),
        P(rows, None, cols),
    )

    return jax.shard_map(
        on_device, mesh=fine, in_specs=placed, out_specs=P(rows, cols), check_vma=False
    )
```

```python
import jax
import jax.numpy as jnp
from jax import lax
from jax.experimental import pallas as pl
from jax.experimental.pallas import tpu as pltpu
from jax.sharding import Mesh
from jax.sharding import PartitionSpec as P


EXPERTS = 4
CAP = 48
LOCAL = ("zl", "core")
TILE = 256
GRANT = 16 << 20


def shift(array, axis, step):
    size = lax.axis_size(axis)
    return lax.ppermute(array, axis, [(i, (i + step) % size) for i in range(size)])


def beside(weight):
    return shift(weight, "x", -1), shift(weight, "x", 1)


def across(pair):
    after, before = pair
    half = after.shape[0] // 2
    return shift(after[:half], "x", -1), shift(before[half:], "x", 1)


def project_kernel(rows_ref, own_ref, after_ref, before_ref, *rest):
    *opposite_refs, out_ref, held, sems = rest
    sources, blocks, cap, depth = rows_ref.shape
    tiles = out_ref.shape[1] // TILE
    part = tiles // len(opposite_refs)
    copies = []
    for tile in range(tiles):
        near = pl.ds(tile * TILE, TILE)
        opposite = opposite_refs[tile // part].at[pl.ds(tile % part * TILE, TILE), :]
        views = (own_ref.at[near, :], after_ref.at[near, :], opposite, before_ref.at[near, :])
        copies.append(
            [
                pltpu.make_async_copy(view, held.at[tile, step], sems.at[tile, step])
                for step, view in enumerate(views)
            ]
        )
        for copy in copies[-1]:
            copy.start()
    for tile in range(tiles):
        total = None
        for step in range(blocks):
            copies[tile][step].wait()
            term = lax.dot_general(
                rows_ref[:, step].reshape(sources * cap, depth),
                held[tile, step],
                (((1,), (1,)), ((), ())),
                preferred_element_type=jnp.float32,
            )
            term = term.astype(jnp.bfloat16).astype(jnp.float32)
            total = term if total is None else total + term
        out_ref[:, pl.ds(tile * TILE, TILE)] = total.astype(jnp.bfloat16)


def project(rows, own, pair, opposite):
    sources, blocks, cap, depth = rows.shape
    width = own.shape[0]
    vmem = pl.BlockSpec(memory_space=pltpu.VMEM)
    return pl.pallas_call(
        project_kernel,
        out_shape=jax.ShapeDtypeStruct((sources * cap, width), jnp.bfloat16),
        in_specs=[vmem]
        + [pl.BlockSpec(memory_space=pl.ANY)] * 3
        + [pl.BlockSpec(memory_space=pltpu.HBM)] * len(opposite),
        out_specs=vmem,
        scratch_shapes=[
            pltpu.VMEM((width // TILE, blocks, TILE, depth), jnp.bfloat16),
            pltpu.SemaphoreType.DMA((width // TILE, blocks)),
        ],
        compiler_params=pltpu.CompilerParams(vmem_limit_bytes=GRANT),
        cost_estimate=pl.CostEstimate(
            flops=2 * sources * cap * blocks * depth * width,
            bytes_accessed=2 * (rows.size + blocks * own.size + sources * cap * width),
            transcendentals=0,
        ),
    )(rows, own, *pair, *opposite)


def expand_kernel(order_ref, hidden_ref, own_ref, after_ref, before_ref, across_ref, out_ref):
    sources, _, cap, width = out_ref.shape
    hidden = hidden_ref[...]
    for step, block in ((0, own_ref), (1, after_ref), (3, before_ref), (2, across_ref)):
        term = jnp.dot(hidden, block[...], preferred_element_type=jnp.float32)
        out_ref[:, order_ref[step]] = term.astype(jnp.bfloat16).reshape(sources, cap, width)


def expand(order, hidden, own, pair, opposite, sources):
    rows, width = hidden.shape
    depth = own.shape[1]
    cap = rows // sources
    places = order.shape[0]
    vmem = pl.BlockSpec(memory_space=pltpu.VMEM)
    return pl.pallas_call(
        expand_kernel,
        out_shape=jax.ShapeDtypeStruct((sources, places, cap, depth), jnp.bfloat16),
        in_specs=[pl.BlockSpec(memory_space=pltpu.SMEM)] + [vmem] * 5,
        out_specs=vmem,
        compiler_params=pltpu.CompilerParams(vmem_limit_bytes=GRANT),
        cost_estimate=pl.CostEstimate(
            flops=2 * rows * width * depth * places,
            bytes_accessed=2 * (hidden.size + places * own.size + places * rows * depth),
            transcendentals=0,
        ),
    )(order, hidden, own, *pair, *opposite)


def on_device(tokens, expert_ids, gate_fixed, w_gate, w_up, w_down):
    width_part = tokens.shape[1]
    x_size = lax.axis_size("x")
    y_size = lax.axis_size("y")
    zh_size = lax.axis_size("zh")
    x_own = lax.axis_index("x")
    expert_iota = jnp.arange(EXPERTS, dtype=jnp.int32)
    matched = expert_ids[:, :, None] == expert_iota
    routed = jnp.sum(matched.astype(jnp.int32), axis=1)
    weights = (
        jnp.sum(jnp.where(matched, gate_fixed[:, :, None], 0), axis=1).astype(jnp.float32) / 65536.0
    )
    position = jnp.cumsum(routed, axis=0) - routed
    slot_iota = jnp.arange(CAP, dtype=jnp.int32)
    placed = (position[:, :, None] == slot_iota) & (routed[:, :, None] > 0)
    outgoing = jnp.einsum(
        "tec,td->ecd", placed.astype(jnp.bfloat16), tokens, preferred_element_type=jnp.float32
    ).astype(jnp.bfloat16)
    sent = jnp.broadcast_to(outgoing[:, None], (EXPERTS, x_size, CAP, width_part))
    local = lax.all_to_all(
        sent.reshape(EXPERTS * x_size, CAP, width_part),
        LOCAL + ("x",),
        split_axis=0,
        concat_axis=0,
        tiled=True,
    ).reshape(EXPERTS, x_size, CAP, width_part)
    order = [(x_own + step) % x_size for step in range(x_size)]
    mine = lax.dynamic_index_in_dim(local, x_own, 0, keepdims=False)
    mine = jnp.stack([lax.dynamic_index_in_dim(mine, place, 0, keepdims=False) for place in order])
    sent_y = jnp.broadcast_to(mine[None], (y_size, x_size, CAP, width_part))
    rows = lax.all_to_all(sent_y, "y", split_axis=0, concat_axis=0, tiled=True)
    total_rows = y_size * CAP

    gate_own = w_gate[0]
    gate_pair = beside(gate_own)
    gate_halves = across(gate_pair)
    up_own, _ = lax.optimization_barrier((w_up[0], gate_pair))
    up_pair = beside(up_own)
    up_last, _ = lax.optimization_barrier((w_up[0], gate_halves))
    up_across = (shift(up_last, "x", 2),)

    def share(term):
        parts = lax.all_to_all(term, "zh", split_axis=0, concat_axis=0, tiled=True)
        parts = parts.reshape(zh_size, total_rows // zh_size, -1)
        return jnp.sum(parts.astype(jnp.float32), axis=0)

    gate_term = project(rows, gate_own, gate_pair, gate_halves)
    gate_share = share(gate_term)
    up_term = project(rows, up_own, up_pair, up_across)
    down_own, up_term = lax.optimization_barrier((w_down[0], up_term))
    down_pair = beside(down_own)
    down_across = (shift(down_own, "x", 2),)
    up_share = share(up_term)
    hidden = (jax.nn.silu(gate_share) * up_share).astype(jnp.bfloat16)
    hidden_rows = lax.all_gather(hidden, "zh", axis=0, tiled=True)
    back = expand(jnp.stack(order), hidden_rows, down_own, down_pair, down_across, y_size)
    back = lax.all_to_all(
        back.reshape(y_size * x_size, CAP, width_part),
        ("y", "x"),
        split_axis=0,
        concat_axis=0,
        tiled=True,
    ).reshape(y_size, x_size, CAP, width_part)
    back = jnp.sum(back.astype(jnp.float32), axis=0).astype(jnp.bfloat16)
    summed = lax.all_to_all(back, LOCAL, split_axis=0, concat_axis=0, tiled=True)
    summed = summed.astype(jnp.float32)
    selector = placed.astype(jnp.float32) * weights[:, :, None]
    mixed = jnp.einsum("tec,ecd->td", selector, summed, precision=lax.Precision.HIGHEST)
    return mixed.astype(jnp.bfloat16)


def solution(mesh):
    expert, tensor = mesh.devices.shape
    fine = Mesh(
        mesh.devices.reshape(expert // 4, 2, 2, 4, tensor // 4), ("y", "zl", "core", "x", "zh")
    )
    rows, cols = ("y", "zl", "core"), ("x", "zh")
    placed = (
        P(rows, cols),
        P(rows, None),
        P(rows, None),
        P(rows, None, cols),
        P(rows, None, cols),
        P(rows, None, cols),
    )

    return jax.shard_map(
        on_device, mesh=fine, in_specs=placed, out_specs=P(rows, cols), check_vma=False
    )
```

```python
import jax
import jax.numpy as jnp
from jax import lax
from jax.experimental import pallas as pl
from jax.experimental.pallas import tpu as pltpu
from jax.sharding import Mesh
from jax.sharding import PartitionSpec as P


EXPERTS = 4
CAP = 48
LOCAL = ("zl", "core")
TILE = 256
GRANT = 16 << 20


def shift(array, axis, step):
    size = lax.axis_size(axis)
    return lax.ppermute(array, axis, [(i, (i + step) % size) for i in range(size)])


def beside(weight):
    return shift(weight, "x", -1), shift(weight, "x", 1)


def across(pair):
    after, before = pair
    half = after.shape[0] // 2
    return shift(after[:half], "x", -1), shift(before[half:], "x", 1)


def block_term(rows_ref, step, block):
    sources, _, cap, depth = rows_ref.shape
    term = lax.dot_general(
        rows_ref[:, step].reshape(sources * cap, depth),
        block,
        (((1,), (1,)), ((), ())),
        preferred_element_type=jnp.float32,
    )
    return term.astype(jnp.bfloat16).astype(jnp.float32)


def project_kernel(rows_ref, own_ref, after_ref, before_ref, *rest):
    *opposite_refs, out_ref = rest
    width = out_ref.shape[1]
    for start in range(0, width, TILE):
        tile = pl.ds(start, TILE)
        total = block_term(rows_ref, 0, own_ref[tile, :])
        total += block_term(rows_ref, 1, after_ref[tile, :])
        total += block_term(rows_ref, 3, before_ref[tile, :])
        if opposite_refs:
            part = width // len(opposite_refs)
            opposite = opposite_refs[start // part]
            total += block_term(rows_ref, 2, opposite[pl.ds(start % part, TILE), :])
        out_ref[:, tile] = total.astype(out_ref.dtype)


def finish_kernel(rows_ref, total_ref, opposite_ref, out_ref):
    for start in range(0, out_ref.shape[1], TILE):
        tile = pl.ds(start, TILE)
        total = total_ref[:, tile] + block_term(rows_ref, 2, opposite_ref[tile, :])
        out_ref[:, tile] = total.astype(out_ref.dtype)


def project(rows, own, pair, opposite=()):
    width = own.shape[0]
    dtype = jnp.bfloat16 if opposite else jnp.float32
    return product(project_kernel, rows, width, dtype, own, *pair, *opposite)


def finish(rows, total, opposite):
    return product(finish_kernel, rows, opposite.shape[0], jnp.bfloat16, total, opposite)


def product(kernel, rows, width, dtype, *operands):
    sources, _, cap, _ = rows.shape
    used = sum(operand.size for operand in operands)
    vmem = pl.BlockSpec(memory_space=pltpu.VMEM)
    return pl.pallas_call(
        kernel,
        out_shape=jax.ShapeDtypeStruct((sources * cap, width), dtype),
        in_specs=[vmem] * (1 + len(operands)),
        out_specs=vmem,
        compiler_params=pltpu.CompilerParams(vmem_limit_bytes=GRANT),
        cost_estimate=pl.CostEstimate(
            flops=2 * sources * cap * used,
            bytes_accessed=2 * (rows.size + used + sources * cap * width),
            transcendentals=0,
        ),
    )(rows, *operands)


def expand_kernel(order_ref, hidden_ref, own_ref, after_ref, before_ref, across_ref, out_ref):
    sources, _, cap, width = out_ref.shape
    hidden = hidden_ref[...]
    for step, block in ((0, own_ref), (1, after_ref), (3, before_ref), (2, across_ref)):
        term = jnp.dot(hidden, block[...], preferred_element_type=jnp.float32)
        out_ref[:, order_ref[step]] = term.astype(jnp.bfloat16).reshape(sources, cap, width)


def expand(order, hidden, own, pair, opposite, sources):
    rows, width = hidden.shape
    depth = own.shape[1]
    cap = rows // sources
    places = order.shape[0]
    vmem = pl.BlockSpec(memory_space=pltpu.VMEM)
    return pl.pallas_call(
        expand_kernel,
        out_shape=jax.ShapeDtypeStruct((sources, places, cap, depth), jnp.bfloat16),
        in_specs=[pl.BlockSpec(memory_space=pltpu.SMEM)] + [vmem] * 5,
        out_specs=vmem,
        compiler_params=pltpu.CompilerParams(vmem_limit_bytes=GRANT),
        cost_estimate=pl.CostEstimate(
            flops=2 * rows * width * depth * places,
            bytes_accessed=2 * (hidden.size + places * own.size + places * rows * depth),
            transcendentals=0,
        ),
    )(order, hidden, own, *pair, *opposite)


def on_device(tokens, expert_ids, gate_fixed, w_gate, w_up, w_down):
    width_part = tokens.shape[1]
    x_size = lax.axis_size("x")
    y_size = lax.axis_size("y")
    zh_size = lax.axis_size("zh")
    x_own = lax.axis_index("x")
    expert_iota = jnp.arange(EXPERTS, dtype=jnp.int32)
    matched = expert_ids[:, :, None] == expert_iota
    routed = jnp.sum(matched.astype(jnp.int32), axis=1)
    weights = (
        jnp.sum(jnp.where(matched, gate_fixed[:, :, None], 0), axis=1).astype(jnp.float32) / 65536.0
    )
    position = jnp.cumsum(routed, axis=0) - routed
    slot_iota = jnp.arange(CAP, dtype=jnp.int32)
    placed = (position[:, :, None] == slot_iota) & (routed[:, :, None] > 0)
    outgoing = jnp.einsum(
        "tec,td->ecd", placed.astype(jnp.bfloat16), tokens, preferred_element_type=jnp.float32
    ).astype(jnp.bfloat16)
    sent = jnp.broadcast_to(outgoing[:, None], (EXPERTS, x_size, CAP, width_part))
    local = lax.all_to_all(
        sent.reshape(EXPERTS * x_size, CAP, width_part),
        LOCAL + ("x",),
        split_axis=0,
        concat_axis=0,
        tiled=True,
    ).reshape(EXPERTS, x_size, CAP, width_part)
    order = [(x_own + step) % x_size for step in range(x_size)]
    mine = lax.dynamic_index_in_dim(local, x_own, 0, keepdims=False)
    mine = jnp.stack([lax.dynamic_index_in_dim(mine, place, 0, keepdims=False) for place in order])
    sent_y = jnp.broadcast_to(mine[None], (y_size, x_size, CAP, width_part))
    rows = lax.all_to_all(sent_y, "y", split_axis=0, concat_axis=0, tiled=True)
    total_rows = y_size * CAP

    gate_own = w_gate[0]
    gate_pair = beside(gate_own)
    gate_halves = across(gate_pair)
    up_own, _ = lax.optimization_barrier((w_up[0], gate_pair))
    up_pair = beside(up_own)

    def share(term):
        parts = lax.all_to_all(term, "zh", split_axis=0, concat_axis=0, tiled=True)
        parts = parts.reshape(zh_size, total_rows // zh_size, -1)
        return jnp.sum(parts.astype(jnp.float32), axis=0)

    gate_term = project(rows, gate_own, gate_pair, gate_halves)
    up_last, gate_term = lax.optimization_barrier((w_up[0], gate_term))
    up_across = shift(up_last, "x", 2)
    gate_share = share(gate_term)
    up_open = project(rows, up_own, up_pair)
    up_term = finish(rows, up_open, up_across)
    down_own, up_term = lax.optimization_barrier((w_down[0], up_term))
    down_pair = beside(down_own)
    down_across = (shift(down_own, "x", 2),)
    up_share = share(up_term)
    hidden = (jax.nn.silu(gate_share) * up_share).astype(jnp.bfloat16)
    hidden_rows = lax.all_gather(hidden, "zh", axis=0, tiled=True)
    back = expand(jnp.stack(order), hidden_rows, down_own, down_pair, down_across, y_size)
    back = lax.all_to_all(
        back.reshape(y_size * x_size, CAP, width_part),
        ("y", "x"),
        split_axis=0,
        concat_axis=0,
        tiled=True,
    ).reshape(y_size, x_size, CAP, width_part)
    back = jnp.sum(back.astype(jnp.float32), axis=0).astype(jnp.bfloat16)
    summed = lax.all_to_all(back, LOCAL, split_axis=0, concat_axis=0, tiled=True)
    summed = summed.astype(jnp.float32)
    selector = placed.astype(jnp.float32) * weights[:, :, None]
    mixed = jnp.einsum("tec,ecd->td", selector, summed, precision=lax.Precision.HIGHEST)
    return mixed.astype(jnp.bfloat16)


def solution(mesh):
    expert, tensor = mesh.devices.shape
    fine = Mesh(
        mesh.devices.reshape(expert // 4, 2, 2, 4, tensor // 4), ("y", "zl", "core", "x", "zh")
    )
    rows, cols = ("y", "zl", "core"), ("x", "zh")
    placed = (
        P(rows, cols),
        P(rows, None),
        P(rows, None),
        P(rows, None, cols),
        P(rows, None, cols),
        P(rows, None, cols),
    )

    return jax.shard_map(
        on_device, mesh=fine, in_specs=placed, out_specs=P(rows, cols), check_vma=False
    )
```

```python
import functools

import jax
import jax.numpy as jnp
from jax import lax
from jax.experimental import pallas as pl
from jax.experimental.pallas import tpu as pltpu
from jax.sharding import Mesh
from jax.sharding import PartitionSpec as P


EXPERTS = 4
CAP = 48
LOCAL = ("zl", "core")
TILE = 256
GRANT = 16 << 20


def shift(array, axis, step):
    size = lax.axis_size(axis)
    return lax.ppermute(array, axis, [(i, (i + step) % size) for i in range(size)])


def beside(weight):
    return shift(weight, "x", -1), shift(weight, "x", 1)


def across(pair):
    after, before = pair
    half = after.shape[0] // 2
    return shift(after[:half], "x", -1), shift(before[half:], "x", 1)


def block_term(rows_ref, step, block):
    sources, _, cap, depth = rows_ref.shape
    term = lax.dot_general(
        rows_ref[:, step].reshape(sources * cap, depth),
        block,
        (((1,), (1,)), ((), ())),
        preferred_element_type=jnp.float32,
    )
    return term.astype(jnp.bfloat16).astype(jnp.float32)


def project_kernel(steps, rows_ref, *refs):
    *block_refs, out_ref = refs
    width = out_ref.shape[1]
    opened = block_refs.pop(0) if block_refs[0].shape == out_ref.shape else None
    for start in range(0, width, TILE):
        tile = pl.ds(start, TILE)
        total = None if opened is None else opened[:, tile]
        pieces = list(block_refs)
        for step in steps:
            block = pieces.pop(0)
            if block.shape[0] == width:
                block = block[tile, :]
            else:
                other, part = pieces.pop(0), block.shape[0]
                block = (block if start < part else other)[pl.ds(start % part, TILE), :]
            term = block_term(rows_ref, step, block)
            total = term if total is None else total + term
        out_ref[:, tile] = total.astype(out_ref.dtype)


def project(steps, rows, width, dtype, *operands):
    sources, _, cap, _ = rows.shape
    used = sum(operand.size for operand in operands)
    vmem = pl.BlockSpec(memory_space=pltpu.VMEM)
    return pl.pallas_call(
        functools.partial(project_kernel, steps),
        out_shape=jax.ShapeDtypeStruct((sources * cap, width), dtype),
        in_specs=[vmem] * (1 + len(operands)),
        out_specs=vmem,
        compiler_params=pltpu.CompilerParams(vmem_limit_bytes=GRANT),
        cost_estimate=pl.CostEstimate(
            flops=2 * sources * cap * used,
            bytes_accessed=2 * (rows.size + used + sources * cap * width),
            transcendentals=0,
        ),
    )(rows, *operands)


def gate_kernel(rows_ref, after_ref, before_ref, own_ref, low_ref, high_ref, out_ref, own, opposite, sems):
    half = low_ref.shape[0]
    copies = (
        pltpu.make_async_copy(own_ref, own, sems.at[0]),
        pltpu.make_async_copy(low_ref, opposite.at[pl.ds(0, half), :], sems.at[1]),
        pltpu.make_async_copy(high_ref, opposite.at[pl.ds(half, half), :], sems.at[2]),
    )
    for copy in copies:
        copy.start()
    total = block_term(rows_ref, 1, after_ref[...]) + block_term(rows_ref, 3, before_ref[...])
    copies[0].wait()
    total += block_term(rows_ref, 0, own[...])
    copies[1].wait()
    copies[2].wait()
    total += block_term(rows_ref, 2, opposite[...])
    out_ref[...] = total.astype(out_ref.dtype)


def project_gate(rows, own, pair, halves):
    sources, blocks, cap, depth = rows.shape
    width = own.shape[0]
    vmem = pl.BlockSpec(memory_space=pltpu.VMEM)
    anywhere = pl.BlockSpec(memory_space=pl.ANY)
    return pl.pallas_call(
        gate_kernel,
        out_shape=jax.ShapeDtypeStruct((sources * cap, width), jnp.bfloat16),
        in_specs=[vmem] * 3 + [anywhere] * 3,
        out_specs=vmem,
        scratch_shapes=[
            pltpu.VMEM((width, depth), jnp.bfloat16),
            pltpu.VMEM((width, depth), jnp.bfloat16),
            pltpu.SemaphoreType.DMA((3,)),
        ],
        compiler_params=pltpu.CompilerParams(vmem_limit_bytes=GRANT),
        cost_estimate=pl.CostEstimate(
            flops=2 * sources * cap * blocks * own.size,
            bytes_accessed=2 * (rows.size + blocks * own.size + sources * cap * width),
            transcendentals=0,
        ),
    )(rows, *pair, own, *[pltpu.with_memory_space_constraint(half, pltpu.HBM) for half in halves])


def expand_kernel(order_ref, hidden_ref, own_ref, after_ref, before_ref, across_ref, out_ref):
    sources, _, cap, width = out_ref.shape
    hidden = hidden_ref[...]
    for step, block in ((0, own_ref), (1, after_ref), (3, before_ref), (2, across_ref)):
        term = jnp.dot(hidden, block[...], preferred_element_type=jnp.float32)
        out_ref[:, order_ref[step]] = term.astype(jnp.bfloat16).reshape(sources, cap, width)


def expand(order, hidden, own, pair, opposite, sources):
    rows, width = hidden.shape
    depth = own.shape[1]
    cap = rows // sources
    places = order.shape[0]
    vmem = pl.BlockSpec(memory_space=pltpu.VMEM)
    return pl.pallas_call(
        expand_kernel,
        out_shape=jax.ShapeDtypeStruct((sources, places, cap, depth), jnp.bfloat16),
        in_specs=[pl.BlockSpec(memory_space=pltpu.SMEM)] + [vmem] * 5,
        out_specs=vmem,
        compiler_params=pltpu.CompilerParams(vmem_limit_bytes=GRANT),
        cost_estimate=pl.CostEstimate(
            flops=2 * rows * width * depth * places,
            bytes_accessed=2 * (hidden.size + places * own.size + places * rows * depth),
            transcendentals=0,
        ),
    )(order, hidden, own, *pair, *opposite)


def on_device(tokens, expert_ids, gate_fixed, w_gate, w_up, w_down):
    width_part = tokens.shape[1]
    x_size = lax.axis_size("x")
    y_size = lax.axis_size("y")
    zh_size = lax.axis_size("zh")
    x_own = lax.axis_index("x")
    expert_iota = jnp.arange(EXPERTS, dtype=jnp.int32)
    matched = expert_ids[:, :, None] == expert_iota
    routed = jnp.sum(matched.astype(jnp.int32), axis=1)
    weights = (
        jnp.sum(jnp.where(matched, gate_fixed[:, :, None], 0), axis=1).astype(jnp.float32) / 65536.0
    )
    position = jnp.cumsum(routed, axis=0) - routed
    slot_iota = jnp.arange(CAP, dtype=jnp.int32)
    placed = (position[:, :, None] == slot_iota) & (routed[:, :, None] > 0)
    outgoing = jnp.einsum(
        "tec,td->ecd", placed.astype(jnp.bfloat16), tokens, preferred_element_type=jnp.float32
    ).astype(jnp.bfloat16)
    sent = jnp.broadcast_to(outgoing[:, None], (EXPERTS, x_size, CAP, width_part))
    local = lax.all_to_all(
        sent.reshape(EXPERTS * x_size, CAP, width_part),
        LOCAL + ("x",),
        split_axis=0,
        concat_axis=0,
        tiled=True,
    ).reshape(EXPERTS, x_size, CAP, width_part)
    order = [(x_own + step) % x_size for step in range(x_size)]
    mine = lax.dynamic_index_in_dim(local, x_own, 0, keepdims=False)
    mine = jnp.stack([lax.dynamic_index_in_dim(mine, place, 0, keepdims=False) for place in order])
    sent_y = jnp.broadcast_to(mine[None], (y_size, x_size, CAP, width_part))
    rows = lax.all_to_all(sent_y, "y", split_axis=0, concat_axis=0, tiled=True)
    total_rows = y_size * CAP

    gate_own = w_gate[0]
    width = gate_own.shape[0]
    gate_pair = beside(gate_own)
    gate_halves = across(gate_pair)
    up_own = w_up[0]
    half = width // 2
    up_low, up_high, _ = lax.optimization_barrier((up_own[:half], up_own[half:], gate_pair))
    after_low = shift(up_low, "x", -1)
    before_high = shift(up_high, "x", 1)
    after_high = shift(up_high, "x", -1)
    before_low = shift(up_low, "x", 1)
    up_across = shift(after_low, "x", -1), shift(before_high, "x", 1)
    down_last, _ = lax.optimization_barrier((w_down[0], up_across[0]))
    down_across = (shift(down_last, "x", 2),)

    def share(term):
        parts = lax.all_to_all(term, "zh", split_axis=0, concat_axis=0, tiled=True)
        parts = parts.reshape(zh_size, total_rows // zh_size, -1)
        return jnp.sum(parts.astype(jnp.float32), axis=0)

    gate_term = project_gate(rows, gate_own, gate_pair, gate_halves)
    gate_share = share(gate_term)
    up_pair = after_low, after_high, before_low, before_high
    up_open = project((0, 1, 3), rows, width, jnp.float32, up_own, *up_pair)
    up_term = project((2,), rows, width, jnp.bfloat16, up_open, *up_across)
    down_own, up_term = lax.optimization_barrier((w_down[0], up_term))
    down_pair = beside(down_own)
    up_share = share(up_term)
    hidden = (jax.nn.silu(gate_share) * up_share).astype(jnp.bfloat16)
    hidden_rows = lax.all_gather(hidden, "zh", axis=0, tiled=True)
    back = expand(jnp.stack(order), hidden_rows, down_own, down_pair, down_across, y_size)
    back = lax.all_to_all(
        back.reshape(y_size * x_size, CAP, width_part),
        ("y", "x"),
        split_axis=0,
        concat_axis=0,
        tiled=True,
    ).reshape(y_size, x_size, CAP, width_part)
    back = jnp.sum(back.astype(jnp.float32), axis=0).astype(jnp.bfloat16)
    summed = lax.all_to_all(back, LOCAL, split_axis=0, concat_axis=0, tiled=True)
    summed = summed.astype(jnp.float32)
    selector = placed.astype(jnp.float32) * weights[:, :, None]
    mixed = jnp.einsum("tec,ecd->td", selector, summed, precision=lax.Precision.HIGHEST)
    return mixed.astype(jnp.bfloat16)


def solution(mesh):
    expert, tensor = mesh.devices.shape
    fine = Mesh(
        mesh.devices.reshape(expert // 4, 2, 2, 4, tensor // 4), ("y", "zl", "core", "x", "zh")
    )
    rows, cols = ("y", "zl", "core"), ("x", "zh")
    placed = (
        P(rows, cols),
        P(rows, None),
        P(rows, None),
        P(rows, None, cols),
        P(rows, None, cols),
        P(rows, None, cols),
    )

    return jax.shard_map(
        on_device, mesh=fine, in_specs=placed, out_specs=P(rows, cols), check_vma=False
    )
```

```python
import functools

import jax
import jax.numpy as jnp
from jax import lax
from jax.experimental import pallas as pl
from jax.experimental.pallas import tpu as pltpu
from jax.sharding import Mesh
from jax.sharding import PartitionSpec as P


EXPERTS = 4
CAP = 48
LOCAL = ("zl", "core")
TILE = 256
GRANT = 16 << 20


def shift(array, axis, step):
    size = lax.axis_size(axis)
    return lax.ppermute(array, axis, [(i, (i + step) % size) for i in range(size)])


def beside(weight):
    return shift(weight, "x", -1), shift(weight, "x", 1)


def across(pair):
    after, before = pair
    half = after.shape[0] // 2
    return shift(after[:half], "x", -1), shift(before[half:], "x", 1)


def block_term(rows_ref, step, block):
    sources, _, cap, depth = rows_ref.shape
    term = lax.dot_general(
        rows_ref[:, step].reshape(sources * cap, depth),
        block,
        (((1,), (1,)), ((), ())),
        preferred_element_type=jnp.float32,
    )
    return term.astype(jnp.bfloat16).astype(jnp.float32)


def project_kernel(steps, rows_ref, *refs):
    *block_refs, out_ref = refs
    width = out_ref.shape[1]
    opened = block_refs.pop(0) if block_refs[0].shape == out_ref.shape else None
    for start in range(0, width, TILE):
        tile = pl.ds(start, TILE)
        total = None if opened is None else opened[:, tile]
        pieces = list(block_refs)
        for step in steps:
            block = pieces.pop(0)
            if block.shape[0] == width:
                block = block[tile, :]
            else:
                other, part = pieces.pop(0), block.shape[0]
                block = (block if start < part else other)[pl.ds(start % part, TILE), :]
            term = block_term(rows_ref, step, block)
            total = term if total is None else total + term
        out_ref[:, tile] = total.astype(out_ref.dtype)


def project(steps, rows, width, dtype, *operands):
    sources, _, cap, _ = rows.shape
    used = sum(operand.size for operand in operands)
    vmem = pl.BlockSpec(memory_space=pltpu.VMEM)
    return pl.pallas_call(
        functools.partial(project_kernel, steps),
        out_shape=jax.ShapeDtypeStruct((sources * cap, width), dtype),
        in_specs=[vmem] * (1 + len(operands)),
        out_specs=vmem,
        compiler_params=pltpu.CompilerParams(vmem_limit_bytes=GRANT),
        cost_estimate=pl.CostEstimate(
            flops=2 * sources * cap * used,
            bytes_accessed=2 * (rows.size + used + sources * cap * width),
            transcendentals=0,
        ),
    )(rows, *operands)


def gate_kernel(rows_ref, after_ref, before_ref, own_ref, low_ref, high_ref, out_ref, own, opposite, sems):
    half = low_ref.shape[0]
    copies = (
        pltpu.make_async_copy(own_ref, own, sems.at[0]),
        pltpu.make_async_copy(low_ref, opposite.at[pl.ds(0, half), :], sems.at[1]),
        pltpu.make_async_copy(high_ref, opposite.at[pl.ds(half, half), :], sems.at[2]),
    )
    for copy in copies:
        copy.start()
    total = block_term(rows_ref, 1, after_ref[...]) + block_term(rows_ref, 3, before_ref[...])
    copies[0].wait()
    total += block_term(rows_ref, 0, own[...])
    copies[1].wait()
    copies[2].wait()
    total += block_term(rows_ref, 2, opposite[...])
    out_ref[...] = total.astype(out_ref.dtype)


def project_gate(rows, own, pair, halves):
    sources, blocks, cap, depth = rows.shape
    width = own.shape[0]
    vmem = pl.BlockSpec(memory_space=pltpu.VMEM)
    anywhere = pl.BlockSpec(memory_space=pl.ANY)
    return pl.pallas_call(
        gate_kernel,
        out_shape=jax.ShapeDtypeStruct((sources * cap, width), jnp.bfloat16),
        in_specs=[vmem] * 3 + [anywhere] * 3,
        out_specs=vmem,
        scratch_shapes=[
            pltpu.VMEM((width, depth), jnp.bfloat16),
            pltpu.VMEM((width, depth), jnp.bfloat16),
            pltpu.SemaphoreType.DMA((3,)),
        ],
        compiler_params=pltpu.CompilerParams(vmem_limit_bytes=GRANT),
        cost_estimate=pl.CostEstimate(
            flops=2 * sources * cap * blocks * own.size,
            bytes_accessed=2 * (rows.size + blocks * own.size + sources * cap * width),
            transcendentals=0,
        ),
    )(rows, *pair, own, *[pltpu.with_memory_space_constraint(half, pltpu.HBM) for half in halves])


def expand_kernel(order_ref, hidden_ref, own_ref, after_ref, before_ref, across_ref, out_ref):
    sources, _, cap, width = out_ref.shape
    hidden = hidden_ref[...]
    for step, block in ((0, own_ref), (1, after_ref), (3, before_ref), (2, across_ref)):
        term = jnp.dot(hidden, block[...], preferred_element_type=jnp.float32)
        out_ref[:, order_ref[step]] = term.astype(jnp.bfloat16).reshape(sources, cap, width)


def expand(order, hidden, own, pair, opposite, sources):
    rows, width = hidden.shape
    depth = own.shape[1]
    cap = rows // sources
    places = order.shape[0]
    vmem = pl.BlockSpec(memory_space=pltpu.VMEM)
    return pl.pallas_call(
        expand_kernel,
        out_shape=jax.ShapeDtypeStruct((sources, places, cap, depth), jnp.bfloat16),
        in_specs=[pl.BlockSpec(memory_space=pltpu.SMEM)] + [vmem] * 5,
        out_specs=vmem,
        compiler_params=pltpu.CompilerParams(vmem_limit_bytes=GRANT),
        cost_estimate=pl.CostEstimate(
            flops=2 * rows * width * depth * places,
            bytes_accessed=2 * (hidden.size + places * own.size + places * rows * depth),
            transcendentals=0,
        ),
    )(order, hidden, own, *pair, *opposite)


def on_device(tokens, expert_ids, gate_fixed, w_gate, w_up, w_down):
    width_part = tokens.shape[1]
    x_size = lax.axis_size("x")
    y_size = lax.axis_size("y")
    zh_size = lax.axis_size("zh")
    x_own = lax.axis_index("x")
    expert_iota = jnp.arange(EXPERTS, dtype=jnp.int32)
    matched = expert_ids[:, :, None] == expert_iota
    routed = jnp.sum(matched.astype(jnp.int32), axis=1)
    weights = (
        jnp.sum(jnp.where(matched, gate_fixed[:, :, None], 0), axis=1).astype(jnp.float32) / 65536.0
    )
    position = jnp.cumsum(routed, axis=0) - routed
    slot_iota = jnp.arange(CAP, dtype=jnp.int32)
    placed = (position[:, :, None] == slot_iota) & (routed[:, :, None] > 0)
    outgoing = jnp.einsum(
        "tec,td->ecd", placed.astype(jnp.bfloat16), tokens, preferred_element_type=jnp.float32
    ).astype(jnp.bfloat16)
    sent = jnp.broadcast_to(outgoing[:, None], (EXPERTS, x_size, CAP, width_part))
    local = lax.all_to_all(
        sent.reshape(EXPERTS * x_size, CAP, width_part),
        LOCAL + ("x",),
        split_axis=0,
        concat_axis=0,
        tiled=True,
    ).reshape(EXPERTS, x_size, CAP, width_part)
    order = [(x_own + step) % x_size for step in range(x_size)]
    mine = lax.dynamic_index_in_dim(local, x_own, 0, keepdims=False)
    mine = jnp.stack([lax.dynamic_index_in_dim(mine, place, 0, keepdims=False) for place in order])
    sent_y = jnp.broadcast_to(mine[None], (y_size, x_size, CAP, width_part))
    rows = lax.all_to_all(sent_y, "y", split_axis=0, concat_axis=0, tiled=True)
    total_rows = y_size * CAP

    gate_own = w_gate[0]
    width = gate_own.shape[0]
    gate_pair = beside(gate_own)
    gate_halves = across(gate_pair)
    up_own, _ = lax.optimization_barrier((w_up[0], gate_pair))
    up_pair = beside(up_own)
    up_across = across(up_pair)

    def share(term):
        parts = lax.all_to_all(term, "zh", split_axis=0, concat_axis=0, tiled=True)
        parts = parts.reshape(zh_size, total_rows // zh_size, -1)
        return jnp.sum(parts.astype(jnp.float32), axis=0)

    gate_term = project_gate(rows, gate_own, gate_pair, gate_halves)
    gate_share = share(gate_term)
    up_open = project((0, 1, 3), rows, width, jnp.float32, up_own, *up_pair)
    up_term = project((2,), rows, width, jnp.bfloat16, up_open, *up_across)
    down_own, up_term = lax.optimization_barrier((w_down[0], up_term))
    down_pair = beside(down_own)
    down_across = (shift(down_own, "x", 2),)
    up_share = share(up_term)
    hidden = (jax.nn.silu(gate_share) * up_share).astype(jnp.bfloat16)
    hidden_rows = lax.all_gather(hidden, "zh", axis=0, tiled=True)
    back = expand(jnp.stack(order), hidden_rows, down_own, down_pair, down_across, y_size)
    back = lax.all_to_all(
        back.reshape(y_size * x_size, CAP, width_part),
        ("y", "x"),
        split_axis=0,
        concat_axis=0,
        tiled=True,
    ).reshape(y_size, x_size, CAP, width_part)
    back = jnp.sum(back.astype(jnp.float32), axis=0).astype(jnp.bfloat16)
    summed = lax.all_to_all(back, LOCAL, split_axis=0, concat_axis=0, tiled=True)
    summed = summed.astype(jnp.float32)
    selector = placed.astype(jnp.float32) * weights[:, :, None]
    mixed = jnp.einsum("tec,ecd->td", selector, summed, precision=lax.Precision.HIGHEST)
    return mixed.astype(jnp.bfloat16)


def solution(mesh):
    expert, tensor = mesh.devices.shape
    fine = Mesh(
        mesh.devices.reshape(expert // 4, 2, 2, 4, tensor // 4), ("y", "zl", "core", "x", "zh")
    )
    rows, cols = ("y", "zl", "core"), ("x", "zh")
    placed = (
        P(rows, cols),
        P(rows, None),
        P(rows, None),
        P(rows, None, cols),
        P(rows, None, cols),
        P(rows, None, cols),
    )

    return jax.shard_map(
        on_device, mesh=fine, in_specs=placed, out_specs=P(rows, cols), check_vma=False
    )
```

```python
import functools

import jax
import jax.numpy as jnp
from jax import lax
from jax.experimental import pallas as pl
from jax.experimental.pallas import tpu as pltpu
from jax.sharding import Mesh
from jax.sharding import PartitionSpec as P


EXPERTS = 4
CAP = 48
LOCAL = ("zl", "core")
TILE = 256
GRANT = 16 << 20


def shift(array, axis, step):
    size = lax.axis_size(axis)
    return lax.ppermute(array, axis, [(i, (i + step) % size) for i in range(size)])


def turn(array, back):
    size = lax.axis_size("x")
    pairs = []
    for core in range(2):
        step = 1 if (core == 0) == back else -1
        pairs += [(core * size + i, core * size + (i + step) % size) for i in range(size)]
    return lax.ppermute(array, ("core", "x"), pairs)


def beside(weight):
    return turn(weight, False), turn(weight, True)


def across(pair):
    return (turn(pair[0], False),)


def block_term(rows_ref, step, block):
    sources, _, cap, depth = rows_ref.shape
    term = lax.dot_general(
        rows_ref[:, step].reshape(sources * cap, depth),
        block,
        (((1,), (1,)), ((), ())),
        preferred_element_type=jnp.float32,
    )
    return term.astype(jnp.bfloat16).astype(jnp.float32)


def project_kernel(steps, rows_ref, *refs):
    *block_refs, out_ref = refs
    width = out_ref.shape[1]
    opened = block_refs.pop(0) if block_refs[0].shape == out_ref.shape else None
    for start in range(0, width, TILE):
        tile = pl.ds(start, TILE)
        total = None if opened is None else opened[:, tile]
        for step, block in zip(steps, block_refs):
            block = block[tile, :]
            term = block_term(rows_ref, step, block)
            total = term if total is None else total + term
        out_ref[:, tile] = total.astype(out_ref.dtype)


def project(steps, rows, width, dtype, *operands):
    sources, _, cap, _ = rows.shape
    used = sum(operand.size for operand in operands)
    vmem = pl.BlockSpec(memory_space=pltpu.VMEM)
    return pl.pallas_call(
        functools.partial(project_kernel, steps),
        out_shape=jax.ShapeDtypeStruct((sources * cap, width), dtype),
        in_specs=[vmem] * (1 + len(operands)),
        out_specs=vmem,
        compiler_params=pltpu.CompilerParams(vmem_limit_bytes=GRANT),
        cost_estimate=pl.CostEstimate(
            flops=2 * sources * cap * used,
            bytes_accessed=2 * (rows.size + used + sources * cap * width),
            transcendentals=0,
        ),
    )(rows, *operands)


def gate_kernel(rows_ref, after_ref, before_ref, own_ref, across_ref, out_ref, own, opposite, sems):
    copies = (
        pltpu.make_async_copy(own_ref, own, sems.at[0]),
        pltpu.make_async_copy(across_ref, opposite, sems.at[1]),
    )
    for copy in copies:
        copy.start()
    total = block_term(rows_ref, 1, after_ref[...]) + block_term(rows_ref, 3, before_ref[...])
    copies[0].wait()
    total += block_term(rows_ref, 0, own[...])
    copies[1].wait()
    total += block_term(rows_ref, 2, opposite[...])
    out_ref[...] = total.astype(out_ref.dtype)


def project_gate(rows, own, pair, opposite):
    sources, blocks, cap, depth = rows.shape
    width = own.shape[0]
    vmem = pl.BlockSpec(memory_space=pltpu.VMEM)
    anywhere = pl.BlockSpec(memory_space=pl.ANY)
    return pl.pallas_call(
        gate_kernel,
        out_shape=jax.ShapeDtypeStruct((sources * cap, width), jnp.bfloat16),
        in_specs=[vmem] * 3 + [anywhere] * 2,
        out_specs=vmem,
        scratch_shapes=[
            pltpu.VMEM((width, depth), jnp.bfloat16),
            pltpu.VMEM((width, depth), jnp.bfloat16),
            pltpu.SemaphoreType.DMA((2,)),
        ],
        compiler_params=pltpu.CompilerParams(vmem_limit_bytes=GRANT),
        cost_estimate=pl.CostEstimate(
            flops=2 * sources * cap * blocks * own.size,
            bytes_accessed=2 * (rows.size + blocks * own.size + sources * cap * width),
            transcendentals=0,
        ),
    )(rows, *pair, own, pltpu.with_memory_space_constraint(opposite[0], pltpu.HBM))


def expand_kernel(order_ref, hidden_ref, own_ref, after_ref, before_ref, across_ref, out_ref):
    sources, _, cap, width = out_ref.shape
    hidden = hidden_ref[...]
    for step, block in ((0, own_ref), (1, after_ref), (3, before_ref), (2, across_ref)):
        term = jnp.dot(hidden, block[...], preferred_element_type=jnp.float32)
        out_ref[:, order_ref[step]] = term.astype(jnp.bfloat16).reshape(sources, cap, width)


def expand(order, hidden, own, pair, opposite, sources):
    rows, width = hidden.shape
    depth = own.shape[1]
    cap = rows // sources
    places = order.shape[0]
    vmem = pl.BlockSpec(memory_space=pltpu.VMEM)
    return pl.pallas_call(
        expand_kernel,
        out_shape=jax.ShapeDtypeStruct((sources, places, cap, depth), jnp.bfloat16),
        in_specs=[pl.BlockSpec(memory_space=pltpu.SMEM)] + [vmem] * 5,
        out_specs=vmem,
        compiler_params=pltpu.CompilerParams(vmem_limit_bytes=GRANT),
        cost_estimate=pl.CostEstimate(
            flops=2 * rows * width * depth * places,
            bytes_accessed=2 * (hidden.size + places * own.size + places * rows * depth),
            transcendentals=0,
        ),
    )(order, hidden, own, *pair, *opposite)


def on_device(tokens, expert_ids, gate_fixed, w_gate, w_up, w_down):
    width_part = tokens.shape[1]
    x_size = lax.axis_size("x")
    y_size = lax.axis_size("y")
    zh_size = lax.axis_size("zh")
    x_own = lax.axis_index("x")
    expert_iota = jnp.arange(EXPERTS, dtype=jnp.int32)
    matched = expert_ids[:, :, None] == expert_iota
    routed = jnp.sum(matched.astype(jnp.int32), axis=1)
    weights = (
        jnp.sum(jnp.where(matched, gate_fixed[:, :, None], 0), axis=1).astype(jnp.float32) / 65536.0
    )
    position = jnp.cumsum(routed, axis=0) - routed
    slot_iota = jnp.arange(CAP, dtype=jnp.int32)
    placed = (position[:, :, None] == slot_iota) & (routed[:, :, None] > 0)
    outgoing = jnp.einsum(
        "tec,td->ecd", placed.astype(jnp.bfloat16), tokens, preferred_element_type=jnp.float32
    ).astype(jnp.bfloat16)
    sent = jnp.broadcast_to(outgoing[:, None], (EXPERTS, x_size, CAP, width_part))
    local = lax.all_to_all(
        sent.reshape(EXPERTS * x_size, CAP, width_part),
        LOCAL + ("x",),
        split_axis=0,
        concat_axis=0,
        tiled=True,
    ).reshape(EXPERTS, x_size, CAP, width_part)
    sign = 1 - 2 * lax.axis_index("core")
    order = [(x_own + x_size + sign * step) % x_size for step in range(x_size)]
    mine = lax.dynamic_index_in_dim(local, x_own, 0, keepdims=False)
    mine = jnp.stack([lax.dynamic_index_in_dim(mine, place, 0, keepdims=False) for place in order])
    sent_y = jnp.broadcast_to(mine[None], (y_size, x_size, CAP, width_part))
    rows = lax.all_to_all(sent_y, "y", split_axis=0, concat_axis=0, tiled=True)
    total_rows = y_size * CAP

    gate_own = w_gate[0]
    width = gate_own.shape[0]
    gate_pair = beside(gate_own)
    gate_across = across(gate_pair)
    up_own, _ = lax.optimization_barrier((w_up[0], gate_pair))
    up_pair = beside(up_own)
    up_across = across(up_pair)

    def share(term):
        parts = lax.all_to_all(term, "zh", split_axis=0, concat_axis=0, tiled=True)
        parts = parts.reshape(zh_size, total_rows // zh_size, -1)
        return jnp.sum(parts.astype(jnp.float32), axis=0)

    gate_term = project_gate(rows, gate_own, gate_pair, gate_across)
    gate_share = share(gate_term)
    up_open = project((0, 1, 3), rows, width, jnp.float32, up_own, *up_pair)
    up_term = project((2,), rows, width, jnp.bfloat16, up_open, *up_across)
    down_own, up_term = lax.optimization_barrier((w_down[0], up_term))
    down_pair = beside(down_own)
    down_across = (shift(down_own, "x", 2),)
    up_share = share(up_term)
    hidden = (jax.nn.silu(gate_share) * up_share).astype(jnp.bfloat16)
    hidden_rows = lax.all_gather(hidden, "zh", axis=0, tiled=True)
    back = expand(jnp.stack(order), hidden_rows, down_own, down_pair, down_across, y_size)
    back = lax.all_to_all(
        back.reshape(y_size * x_size, CAP, width_part),
        ("y", "x"),
        split_axis=0,
        concat_axis=0,
        tiled=True,
    ).reshape(y_size, x_size, CAP, width_part)
    back = jnp.sum(back.astype(jnp.float32), axis=0).astype(jnp.bfloat16)
    summed = lax.all_to_all(back, LOCAL, split_axis=0, concat_axis=0, tiled=True)
    summed = summed.astype(jnp.float32)
    selector = placed.astype(jnp.float32) * weights[:, :, None]
    mixed = jnp.einsum("tec,ecd->td", selector, summed, precision=lax.Precision.HIGHEST)
    return mixed.astype(jnp.bfloat16)


def solution(mesh):
    expert, tensor = mesh.devices.shape
    fine = Mesh(
        mesh.devices.reshape(expert // 4, 2, 2, 4, tensor // 4), ("y", "zl", "core", "x", "zh")
    )
    rows, cols = ("y", "zl", "core"), ("x", "zh")
    placed = (
        P(rows, cols),
        P(rows, None),
        P(rows, None),
        P(rows, None, cols),
        P(rows, None, cols),
        P(rows, None, cols),
    )

    return jax.shard_map(
        on_device, mesh=fine, in_specs=placed, out_specs=P(rows, cols), check_vma=False
    )
```

```python
import functools

import jax
import jax.numpy as jnp
from jax import lax
from jax.experimental import pallas as pl
from jax.experimental.pallas import tpu as pltpu
from jax.sharding import Mesh
from jax.sharding import PartitionSpec as P


EXPERTS = 4
CAP = 48
LOCAL = ("zl", "core")
TILE = 256
GRANT = 16 << 20


def shift(array, axis, step):
    size = lax.axis_size(axis)
    return lax.ppermute(array, axis, [(i, (i + step) % size) for i in range(size)])


def turn(array, back):
    size = lax.axis_size("x")
    pairs = []
    for core in range(2):
        step = 1 if (core == 0) == back else -1
        pairs += [(core * size + i, core * size + (i + step) % size) for i in range(size)]
    return lax.ppermute(array, ("core", "x"), pairs)


def beside(weight):
    return turn(weight, False), turn(weight, True)


def across(pair):
    return (turn(pair[0], False),)


def across_halves(pair):
    half = pair[0].shape[0] // 2
    return turn(pair[0][:half], False), turn(pair[1][half:], True)


def block_term(rows_ref, step, block):
    sources, _, cap, depth = rows_ref.shape
    term = lax.dot_general(
        rows_ref[:, step].reshape(sources * cap, depth),
        block,
        (((1,), (1,)), ((), ())),
        preferred_element_type=jnp.float32,
    )
    return term.astype(jnp.bfloat16).astype(jnp.float32)


def project_kernel(steps, rows_ref, *refs):
    *block_refs, out_ref = refs
    width = out_ref.shape[1]
    opened = block_refs.pop(0) if block_refs[0].shape == out_ref.shape else None
    for start in range(0, width, TILE):
        tile = pl.ds(start, TILE)
        total = None if opened is None else opened[:, tile]
        for step, block in zip(steps, block_refs):
            block = block[tile, :]
            term = block_term(rows_ref, step, block)
            total = term if total is None else total + term
        out_ref[:, tile] = total.astype(out_ref.dtype)


def project(steps, rows, width, dtype, *operands):
    sources, _, cap, _ = rows.shape
    used = sum(operand.size for operand in operands)
    vmem = pl.BlockSpec(memory_space=pltpu.VMEM)
    return pl.pallas_call(
        functools.partial(project_kernel, steps),
        out_shape=jax.ShapeDtypeStruct((sources * cap, width), dtype),
        in_specs=[vmem] * (1 + len(operands)),
        out_specs=vmem,
        compiler_params=pltpu.CompilerParams(vmem_limit_bytes=GRANT),
        cost_estimate=pl.CostEstimate(
            flops=2 * sources * cap * used,
            bytes_accessed=2 * (rows.size + used + sources * cap * width),
            transcendentals=0,
        ),
    )(rows, *operands)


def gate_kernel(rows_ref, after_ref, before_ref, own_ref, low_ref, high_ref, out_ref, own, opposite, sems):
    half = low_ref.shape[0]
    copies = (
        pltpu.make_async_copy(own_ref, own, sems.at[0]),
        pltpu.make_async_copy(low_ref, opposite.at[pl.ds(0, half), :], sems.at[1]),
        pltpu.make_async_copy(high_ref, opposite.at[pl.ds(half, half), :], sems.at[2]),
    )
    for copy in copies:
        copy.start()
    total = block_term(rows_ref, 1, after_ref[...]) + block_term(rows_ref, 3, before_ref[...])
    copies[0].wait()
    total += block_term(rows_ref, 0, own[...])
    copies[1].wait()
    copies[2].wait()
    total += block_term(rows_ref, 2, opposite[...])
    out_ref[...] = total.astype(out_ref.dtype)


def project_gate(rows, own, pair, halves):
    sources, blocks, cap, depth = rows.shape
    width = own.shape[0]
    vmem = pl.BlockSpec(memory_space=pltpu.VMEM)
    anywhere = pl.BlockSpec(memory_space=pl.ANY)
    return pl.pallas_call(
        gate_kernel,
        out_shape=jax.ShapeDtypeStruct((sources * cap, width), jnp.bfloat16),
        in_specs=[vmem] * 3 + [anywhere] * 3,
        out_specs=vmem,
        scratch_shapes=[
            pltpu.VMEM((width, depth), jnp.bfloat16),
            pltpu.VMEM((width, depth), jnp.bfloat16),
            pltpu.SemaphoreType.DMA((3,)),
        ],
        compiler_params=pltpu.CompilerParams(vmem_limit_bytes=GRANT),
        cost_estimate=pl.CostEstimate(
            flops=2 * sources * cap * blocks * own.size,
            bytes_accessed=2 * (rows.size + blocks * own.size + sources * cap * width),
            transcendentals=0,
        ),
    )(rows, *pair, own, *[pltpu.with_memory_space_constraint(half, pltpu.HBM) for half in halves])


def expand_kernel(order_ref, hidden_ref, own_ref, after_ref, before_ref, across_ref, out_ref):
    sources, _, cap, width = out_ref.shape
    hidden = hidden_ref[...]
    for step, block in ((0, own_ref), (1, after_ref), (3, before_ref), (2, across_ref)):
        term = jnp.dot(hidden, block[...], preferred_element_type=jnp.float32)
        out_ref[:, order_ref[step]] = term.astype(jnp.bfloat16).reshape(sources, cap, width)


def expand(order, hidden, own, pair, opposite, sources):
    rows, width = hidden.shape
    depth = own.shape[1]
    cap = rows // sources
    places = order.shape[0]
    vmem = pl.BlockSpec(memory_space=pltpu.VMEM)
    return pl.pallas_call(
        expand_kernel,
        out_shape=jax.ShapeDtypeStruct((sources, places, cap, depth), jnp.bfloat16),
        in_specs=[pl.BlockSpec(memory_space=pltpu.SMEM)] + [vmem] * 5,
        out_specs=vmem,
        compiler_params=pltpu.CompilerParams(vmem_limit_bytes=GRANT),
        cost_estimate=pl.CostEstimate(
            flops=2 * rows * width * depth * places,
            bytes_accessed=2 * (hidden.size + places * own.size + places * rows * depth),
            transcendentals=0,
        ),
    )(order, hidden, own, *pair, *opposite)


def on_device(tokens, expert_ids, gate_fixed, w_gate, w_up, w_down):
    width_part = tokens.shape[1]
    x_size = lax.axis_size("x")
    y_size = lax.axis_size("y")
    zh_size = lax.axis_size("zh")
    x_own = lax.axis_index("x")
    expert_iota = jnp.arange(EXPERTS, dtype=jnp.int32)
    matched = expert_ids[:, :, None] == expert_iota
    routed = jnp.sum(matched.astype(jnp.int32), axis=1)
    weights = (
        jnp.sum(jnp.where(matched, gate_fixed[:, :, None], 0), axis=1).astype(jnp.float32) / 65536.0
    )
    position = jnp.cumsum(routed, axis=0) - routed
    slot_iota = jnp.arange(CAP, dtype=jnp.int32)
    placed = (position[:, :, None] == slot_iota) & (routed[:, :, None] > 0)
    outgoing = jnp.einsum(
        "tec,td->ecd", placed.astype(jnp.bfloat16), tokens, preferred_element_type=jnp.float32
    ).astype(jnp.bfloat16)
    sent = jnp.broadcast_to(outgoing[:, None], (EXPERTS, x_size, CAP, width_part))
    local = lax.all_to_all(
        sent.reshape(EXPERTS * x_size, CAP, width_part),
        LOCAL + ("x",),
        split_axis=0,
        concat_axis=0,
        tiled=True,
    ).reshape(EXPERTS, x_size, CAP, width_part)
    sign = 1 - 2 * lax.axis_index("core")
    order = [(x_own + x_size + sign * step) % x_size for step in range(x_size)]
    mine = lax.dynamic_index_in_dim(local, x_own, 0, keepdims=False)
    mine = jnp.stack([lax.dynamic_index_in_dim(mine, place, 0, keepdims=False) for place in order])
    sent_y = jnp.broadcast_to(mine[None], (y_size, x_size, CAP, width_part))
    rows = lax.all_to_all(sent_y, "y", split_axis=0, concat_axis=0, tiled=True)
    total_rows = y_size * CAP

    gate_own = w_gate[0]
    width = gate_own.shape[0]
    gate_pair = beside(gate_own)
    gate_across = across_halves(gate_pair)
    up_own, _ = lax.optimization_barrier((w_up[0], gate_pair))
    up_pair = beside(up_own)
    up_across = across(up_pair)

    def share(term):
        parts = lax.all_to_all(term, "zh", split_axis=0, concat_axis=0, tiled=True)
        parts = parts.reshape(zh_size, total_rows // zh_size, -1)
        return jnp.sum(parts.astype(jnp.float32), axis=0)

    gate_term = project_gate(rows, gate_own, gate_pair, gate_across)
    gate_share = share(gate_term)
    up_open = project((0, 1, 3), rows, width, jnp.float32, up_own, *up_pair)
    up_term = project((2,), rows, width, jnp.bfloat16, up_open, *up_across)
    down_own, up_term = lax.optimization_barrier((w_down[0], up_term))
    down_pair = beside(down_own)
    down_across = (shift(down_own, "x", 2),)
    up_share = share(up_term)
    hidden = (jax.nn.silu(gate_share) * up_share).astype(jnp.bfloat16)
    hidden_rows = lax.all_gather(hidden, "zh", axis=0, tiled=True)
    back = expand(jnp.stack(order), hidden_rows, down_own, down_pair, down_across, y_size)
    back = lax.all_to_all(
        back.reshape(y_size * x_size, CAP, width_part),
        ("y", "x"),
        split_axis=0,
        concat_axis=0,
        tiled=True,
    ).reshape(y_size, x_size, CAP, width_part)
    back = jnp.sum(back.astype(jnp.float32), axis=0).astype(jnp.bfloat16)
    summed = lax.all_to_all(back, LOCAL, split_axis=0, concat_axis=0, tiled=True)
    summed = summed.astype(jnp.float32)
    selector = placed.astype(jnp.float32) * weights[:, :, None]
    mixed = jnp.einsum("tec,ecd->td", selector, summed, precision=lax.Precision.HIGHEST)
    return mixed.astype(jnp.bfloat16)


def solution(mesh):
    expert, tensor = mesh.devices.shape
    fine = Mesh(
        mesh.devices.reshape(expert // 4, 2, 2, 4, tensor // 4), ("y", "zl", "core", "x", "zh")
    )
    rows, cols = ("y", "zl", "core"), ("x", "zh")
    placed = (
        P(rows, cols),
        P(rows, None),
        P(rows, None),
        P(rows, None, cols),
        P(rows, None, cols),
        P(rows, None, cols),
    )

    return jax.shard_map(
        on_device, mesh=fine, in_specs=placed, out_specs=P(rows, cols), check_vma=False
    )
```
